256 devices in a mesh: row: 32 (over z_lo, y, core), col: 8 (over x, z_hi).
Axes of the slice: x: 4, y: 4, z: 8 (z_hi: 2, z_lo: 4; z = z_hi * 4 + z_lo), core: 2. Of those that a mesh axis runs over, the one named last changes fastest.
Arguments:
- specimen_slices: float32 [2, 2, 8192, 2048], P(None, None, 'row', 'col'), may hold values from -6 to 6
- illumination_probe: float32 [2, 128, 128], replicated, may hold values from -6 to 6
- propagation_phase: float32 [128, 128], replicated, may hold values from -3.140625 to 3.140625
- amplitudes: float32 [32, 8, 4, 128, 128], P('row', 'col'), may hold values from 0.5 to 4
- positions: int32 [32, 8, 4, 2], P('row', 'col'), may hold values from 0 to 255
- counts: int32 [32, 8], P('row', 'col'), may hold values from 1 to 4, as said below
- measurement_index: int32 [32, 8, 4], P('row', 'col'), may hold values from 0 to 3, each once within a row
Outputs:
- updated: float32 [2, 2, 8192, 2048], P(None, None, 'row', 'col')
The draws below stay inside these ranges and needn't reach their ends.
Inputs may be any that keep to these rules, and one draw needn't show every extreme that they name: `counts`: some tile holds exactly 4 probe positions.
All inputs are finite; a program needn't handle non-finite values.
Results may differ from the reference program's by a relative error of at most 0.0001.
Values sent between devices are 32-bit elements; how exact they have to be, the bound alone decides.
A program may use at most 64 MiB of HBM per device.

```python
import math
import jax
import jax.numpy as jnp
from jax import lax

TILE = 256
PATCH = 128
MAX_PROBE_SPOTS = 4
ITERS = 2
NR = 8192
NC = 2048
N_ROW = 32
N_COL = 8


def draw_counts(key, part):
    rows_tiles = NR // TILE
    cols_tiles = NC // TILE
    key_one, key_two, key_three = jax.random.split(key, 3)
    first = jax.random.randint(key_one, (rows_tiles * cols_tiles,), 1, MAX_PROBE_SPOTS + 1)
    second = jax.random.randint(key_two, (rows_tiles * cols_tiles,), 1, MAX_PROBE_SPOTS + 1)
    values = jnp.minimum(first, second)
    chosen = jax.random.randint(key_three, (), 0, rows_tiles * cols_tiles)
    values = jnp.where(jnp.arange(rows_tiles * cols_tiles) == chosen, MAX_PROBE_SPOTS, values)
    return values.reshape(rows_tiles, cols_tiles).astype(jnp.int32)


def with_ends(entries, rng, smallest, top_value):
    spot = [jax.random.randint(jax.random.fold_in(rng, axis), (), 0, length) for axis, length in enumerate(entries.shape)]
    main_axis = entries.shape.index(max(entries.shape))
    beside = spot[:main_axis] + [(spot[main_axis] + 1) % entries.shape[main_axis]] + spot[main_axis + 1:]
    return entries.at[tuple(spot)].set(smallest).at[tuple(beside)].set(top_value)


def levels(key, shape, pieces, least, largest):
    loudness = 1.0
    for axis_at, parts in pieces:
        heights = jax.random.uniform(jax.random.fold_in(jax.random.fold_in(key, 6), axis_at), (parts,), jnp.float32, least / len(pieces), largest / len(pieces))
        loudness = loudness * jnp.repeat(jnp.exp(heights), shape[axis_at] // parts).reshape((-1,) + (1,) * (len(shape) - 1 - axis_at))
    return loudness


def scatter_about(own_key, shape, scale, reach, shards=(), kind=jnp.bfloat16):
    entries = scale * jax.random.normal(own_key, shape, jnp.float32)
    if shards:
        entries = entries * levels(own_key, shape, shards, -0.22, 0.18)
    return jnp.clip(entries, -reach, reach).astype(kind)


def setup_inputs(seed: int = 0) -> dict:
    arg_keys = jax.random.split(jax.random.key(seed), 8)
    return {
        "specimen_slices": scatter_about(arg_keys[0], (2, 2, NR, NC), 1.0, 6.0, ((2, 32), (3, 8)), jnp.float32),
        "illumination_probe": scatter_about(arg_keys[1], (2, PATCH, PATCH), 1.0, 6.0, (), jnp.float32),
        "propagation_phase": jnp.clip(jax.random.uniform(arg_keys[2], (PATCH, PATCH), jnp.float32, -3.140625, 3.140625), -3.140625, 3.140625),
        "amplitudes": jnp.clip(jnp.exp(math.log(4.0) - 2.0794415 * jax.random.uniform(arg_keys[3], (N_ROW, N_COL, MAX_PROBE_SPOTS, PATCH, PATCH), jnp.float32) ** levels(arg_keys[3], (N_ROW, N_COL, MAX_PROBE_SPOTS, PATCH, PATCH), ((0, 32), (1, 8)), -0.2, 0.2)), 0.5, 4.0),
        "positions": with_ends(jax.random.randint(arg_keys[4], (N_ROW, N_COL, MAX_PROBE_SPOTS, 2), 0, TILE), jax.random.fold_in(arg_keys[4], 1), 0, TILE - 1).astype(jnp.int32),
        "counts": draw_counts(jax.random.fold_in(arg_keys[7], 71), 0),
        "measurement_index": jax.vmap(lambda own: jax.random.permutation(own, MAX_PROBE_SPOTS))(jax.random.split(arg_keys[6], N_ROW * N_COL)).reshape((N_ROW, N_COL, MAX_PROBE_SPOTS)).astype(jnp.int32),
    }


step_size = 0.02
floor_amp = 0.5

def dft_table(width):
    index = jnp.arange(width, dtype=jnp.int32)
    phase_int = index[:, None] * index[None, :] % width
    angle = phase_int.astype(jnp.float32) * (2.0 * math.pi / width)
    scale = 1.0 / math.sqrt(width)
    return (jnp.cos(angle) * scale, -jnp.sin(angle) * scale)

def real_dot(left, right):
    return jnp.dot(left, right, precision=lax.Precision.HIGHEST)

def complex_dot(left, right):
    return (real_dot(left[0], right[0]) - real_dot(left[1], right[1]), real_dot(left[0], right[1]) + real_dot(left[1], right[0]))

def complex_mul(left, right):
    return (left[0] * right[0] - left[1] * right[1], left[0] * right[1] + left[1] * right[0])

def conjugate(pair):
    return (pair[0], -pair[1])

def transform(pair, table, sign):
    matrix = (table[0], sign * table[1])
    return complex_dot(complex_dot(matrix, pair), matrix)

def probe_gradient(windows, probe_pair, prop_pair, recorded_intensity, table):
    first = (windows[0], windows[1])
    second = (windows[2], windows[3])
    exit_one = complex_mul(probe_pair, first)
    moved = transform(complex_mul(prop_pair, transform(exit_one, table, 1.0)), table, -1.0)
    exit_two = complex_mul(moved, second)
    psi_wave = transform(exit_two, table, 1.0)
    magnitude = jnp.sqrt(psi_wave[0] * psi_wave[0] + psi_wave[1] * psi_wave[1])
    factor = 1.0 - recorded_intensity / jnp.maximum(magnitude, floor_amp)
    residual = (psi_wave[0] * factor, psi_wave[1] * factor)
    back_two = transform(residual, table, -1.0)
    grad_two = complex_mul(conjugate(moved), back_two)
    back_moved = complex_mul(conjugate(second), back_two)
    back_one = transform(complex_mul(conjugate(prop_pair), transform(back_moved, table, 1.0)), table, -1.0)
    grad_one = complex_mul(conjugate(probe_pair), back_one)
    return jnp.stack([grad_one[0], grad_one[1], grad_two[0], grad_two[1]])

def reference(specimen_slices, illumination_probe, propagation_phase, amplitudes, positions, counts, measurement_index):
    table = dft_table(PATCH)
    probe_pair = (illumination_probe[0], illumination_probe[1])
    prop_pair = (jnp.cos(propagation_phase), jnp.sin(propagation_phase))
    current = specimen_slices.reshape(4, NR, NC)
    zero_index = jnp.int32(0)
    for iteration in range(ITERS):
        padded = jnp.concatenate([current, current[:, :PATCH, :]], 1)
        padded = jnp.concatenate([padded, padded[:, :, :PATCH]], 2)
        gradient = jnp.zeros_like(padded)

        def per_tile(tile_number, gradient):
            row_of_tile = (tile_number // N_COL).astype(jnp.int32)
            column_of_tile = (tile_number % N_COL).astype(jnp.int32)

            def per_probe(measurement_slot_count, gradient):
                row_start = (row_of_tile * TILE + positions[row_of_tile, column_of_tile, measurement_slot_count, 0]).astype(jnp.int32)
                col_start = (column_of_tile * TILE + positions[row_of_tile, column_of_tile, measurement_slot_count, 1]).astype(jnp.int32)
                windows = lax.dynamic_slice(padded, (zero_index, row_start, col_start), (4, PATCH, PATCH))
                recorded_intensity = amplitudes[row_of_tile, column_of_tile, measurement_index[row_of_tile, column_of_tile, measurement_slot_count]]
                update = probe_gradient(windows, probe_pair, prop_pair, recorded_intensity, table)
                before = lax.dynamic_slice(gradient, (zero_index, row_start, col_start), (4, PATCH, PATCH))
                return lax.dynamic_update_slice(gradient, before + update, (zero_index, row_start, col_start))
            return lax.fori_loop(0, counts[row_of_tile, column_of_tile], per_probe, gradient)
        gradient = lax.fori_loop(0, N_ROW * N_COL, per_tile, gradient)
        folded = gradient[:, :NR, :NC]
        folded = folded.at[:, :PATCH, :].add(gradient[:, NR:, :NC])
        folded = folded.at[:, :, :PATCH].add(gradient[:, :NR, NC:])
        folded = folded.at[:, :PATCH, :PATCH].add(gradient[:, NR:, NC:])
        current = current - step_size * folded
    return current.reshape(2, 2, NR, NC)
```

```python
import math

import jax
import jax.numpy as jnp
import numpy as np
from jax import lax
from jax.experimental import pallas as pl
from jax.experimental.pallas import tpu as pltpu
from jax.sharding import PartitionSpec as P

SLOTS = 4
W = 128
TILE = 256
STEP = 0.02
FLOOR = 0.5
F32 = jnp.float32
BF16 = jnp.bfloat16
MESH = pl.DeviceIdType.MESH


def tables():
    k = np.arange(W)
    angle = (k[:, None] * k[None, :] % W) * (2.0 * math.pi / W)
    re = np.cos(angle) / math.sqrt(W)
    im = -np.sin(angle) / math.sqrt(W)
    forward = np.block([[re, im], [-im, re]]).astype(np.float32)
    backward = np.block([[re, -im], [im, re]]).astype(np.float32)
    both = jnp.asarray(np.stack([forward, backward]))
    high = both.astype(BF16)
    low = (both - high.astype(F32)).astype(BF16)
    return high, low


def split(v):
    high = v.astype(BF16)
    return high, (v - high.astype(F32)).astype(BF16)


def dot(a, b):
    return jnp.dot(a, b, preferred_element_type=F32)


def swap_blocks(v):
    top = jnp.concatenate([v[:W, :W], v[W:, :W]], 1)
    bottom = jnp.concatenate([v[:W, W:], v[W:, W:]], 1)
    return jnp.concatenate([top, bottom], 0)


def transform(v, left, right):
    vh, vl = split(v)
    v = dot(left[0], vh) + (dot(left[1], vh) + dot(left[0], vl))
    vh, vl = split(swap_blocks(v))
    v = dot(vh, right[0]) + (dot(vh, right[1]) + dot(vl, right[0]))
    return swap_blocks(v)


def cmul(a, b):
    ar, ai, br, bi = a[:W], a[W:], b[:W], b[W:]
    return jnp.concatenate([ar * br - ai * bi, ar * bi + ai * br], 0)


def cmul_conj(a, b):
    ar, ai, br, bi = a[:W], a[W:], b[:W], b[W:]
    return jnp.concatenate([ar * br + ai * bi, ar * bi - ai * br], 0)


def kernel(
    pos, cnt, order,
    x, probe_in, phase, amp, th, tl,
    out,
    ea0, ea1, eb0, eb1, ga0, ga1, gb0, gb1,
    rfa0, rfa1, rfb0, rfb1, cla0, cla1, clb0, clb1, cr0, cr1,
    pad, prb, prp, q_s, o2_s, back_s,
    ssem, rsem,
):
    row, col = lax.axis_index("row"), lax.axis_index("col")
    n_row, n_col = lax.axis_size("row"), lax.axis_size("col")
    up = (lax.rem(row + n_row - 1, n_row), col)
    down = (lax.rem(row + 1, n_row), col)
    left = (row, lax.rem(col + n_col - 1, n_col))
    right = (row, lax.rem(col + 1, n_col))
    ext = ((ea0, ea1), (eb0, eb1))
    grad = ((ga0, ga1), (gb0, gb1))
    rfold = ((rfa0, rfa1), (rfb0, rfb1))
    cleft = ((cla0, cla1), (clb0, clb1))
    cright = (cr0, cr1)
    taken = [0]
    started = []

    def send(src, dst, device):
        i = taken[0]
        taken[0] += 1
        copy = pltpu.make_async_remote_copy(
            src_ref=src, dst_ref=dst, send_sem=ssem.at[i], recv_sem=rsem.at[i],
            device_id=device, device_id_type=MESH,
        )
        copy.start()
        started.append(copy)
        return copy

    barrier = pltpu.get_barrier_semaphore()
    for d in (up, down, left, right):
        pl.semaphore_signal(barrier, inc=1, device_id=d, device_id_type=MESH)
    pl.semaphore_wait(barrier, 4)

    lo, hi, all_rows, over = pl.ds(0, W), pl.ds(W, W), pl.ds(0, TILE), pl.ds(TILE, W)

    halo = []
    for s in range(2):
        e = ext[0][s]
        c0 = send(x.at[s, :, lo, lo], e.at[:, 2, lo], left)
        r0 = send(x.at[s, :, lo, lo], e.at[:, 0, over], up)
        r1 = send(x.at[s, :, lo, hi], e.at[:, 1, over], up)
        c1 = send(x.at[s, :, hi, lo], e.at[:, 2, hi], left)
        halo.append((c0, c1, r0, r1))

    for s in range(2):
        for b in range(2):
            ext[0][s][:, b, 0:TILE, :] = x[s, :, :, b * W:(b + 1) * W]
    pad[:, :, :, 0:TILE, :] = jnp.zeros((SLOTS, 2, 3, TILE, W), F32)
    pad[:, :, :, TILE + W:, :] = jnp.zeros((SLOTS, 2, 3, TILE, W), F32)
    for i in range(2):
        p = probe_in[i]
        prb[i * W:(i + 1) * W, :] = jnp.concatenate([p, p], 1)
    cs, sn = jnp.cos(phase[...]), jnp.sin(phase[...])
    prp[0:W, :] = jnp.concatenate([cs, cs], 1)
    prp[W:, :] = jnp.concatenate([sn, sn], 1)

    def corner(s):
        c0, c1, r0, r1 = halo[s]
        e = ext[0][s]
        c0.wait_recv()
        forward = send(e.at[:, 2, lo], e.at[:, 2, over], up)
        for c in (c1, r0, r1, forward):
            c.wait_recv()

    lane = lax.broadcasted_iota(jnp.int32, (W, W), 1)

    def place(j):
        r, c = pos[j, 0], pos[j, 1]
        h = lax.shift_right_logical(c, 7)
        return r, h, c - h * W

    def window(e, j):
        r, h, s = place(j)
        back = lax.rem(W - s, W)
        parts = []
        for i in range(2):
            a = pltpu.roll(e[i, h, pl.ds(r, W), :], back, 1)
            b = pltpu.roll(e[i, h + 1, pl.ds(r, W), :], back, 1)
            parts.append(jnp.where(lane < W - s, a, b))
        return jnp.concatenate(parts, 0)

    def pair_window(e, p):
        return jnp.concatenate([window(e, 2 * p), window(e, 2 * p + 1)], 1)

    def spread(g, p):
        for k in range(2):
            j = 2 * p + k
            r, h, s = place(j)
            live = j < cnt[0]
            for i in range(2):
                v = pltpu.roll(g[i * W:(i + 1) * W, k * W:(k + 1) * W], s, 1)
                v = jnp.where(live, v, 0.0)
                first = jnp.where(lane >= s, v, 0.0)
                second = jnp.where(lane >= s, 0.0, v)
                pad[j, i, 0, over, :] = jnp.where(h == 0, first, 0.0)
                pad[j, i, 1, over, :] = jnp.where(h == 0, second, first)
                pad[j, i, 2, over, :] = jnp.where(h == 0, 0.0, second)

    def collect(g):
        starts = [TILE - place(j)[0] for j in range(SLOTS)]
        for i in range(2):
            for b in range(3):
                v = pad[0, i, b, pl.ds(starts[0], TILE + W), :]
                for j in range(1, SLOTS):
                    v = v + pad[j, i, b, pl.ds(starts[j], TILE + W), :]
                g[i, b] = v

    def fwd(v):
        return transform(v, (th[1], tl[1]), (th[0], tl[0]))

    def bwd(v):
        return transform(v, (th[0], tl[0]), (th[1], tl[1]))

    def phase_a(e):
        for p in range(2):
            v = fwd(cmul(prb[...], pair_window(e, p)))
            q_s[p] = bwd(cmul(prp[...], v))

    def phase_b(e, g):
        for p in range(2):
            o2 = pair_window(e, p)
            o2_s[p] = o2
            psi = fwd(cmul(q_s[p], o2))
            pr, pi = psi[:W], psi[W:]
            m = jnp.concatenate([amp[order[2 * p]], amp[order[2 * p + 1]]], 1)
            f = 1.0 - m / jnp.maximum(jnp.sqrt(pr * pr + pi * pi), FLOOR)
            d2 = bwd(jnp.concatenate([pr * f, pi * f], 0))
            spread(cmul_conj(q_s[p], d2), p)
            back_s[p] = cmul_conj(o2_s[p], d2)
        collect(g)

    def phase_c(g):
        for p in range(2):
            v = bwd(cmul_conj(prp[...], fwd(back_s[p])))
            spread(cmul_conj(prb[...], v), p)
        collect(g)

    def fold_start(t, s):
        g = grad[t][s]
        f = send(g.at[:, :, over], rfold[t][s], down)
        cs = [send(g.at[:, 2, hi], cleft[t][s].at[:, hi], right)]
        if t == 0:
            cs.append(send(g.at[:, 0, hi], cright[s].at[:, hi], left))
        return f, cs

    def fold_next(t, s, f):
        g = grad[t][s]
        f.wait_recv()
        g[:, :, 0:W, :] += rfold[t][s][...]
        cs = [send(g.at[:, 2, lo], cleft[t][s].at[:, lo], right)]
        if t == 0:
            cs.append(send(g.at[:, 0, lo], cright[s].at[:, lo], left))
        return cs

    def update(s, half, cs):
        for c in cs:
            c.wait_recv()
        a, b = half * W, half * W + W
        e, g, n = ext[0][s], grad[0][s], ext[1][s]
        n[:, 0, a:b, :] = e[:, 0, a:b, :] - STEP * (g[:, 0, a:b, :] + cleft[0][s][:, a:b, :])
        n[:, 1, a:b, :] = e[:, 1, a:b, :] - STEP * g[:, 1, a:b, :]
        n[:, 2, a:b, :] = e[:, 2, a:b, :] - STEP * (g[:, 2, a:b, :] + cright[s][:, a:b, :])

    def finish(s, half, cs):
        for c in cs:
            c.wait_recv()
        a, b = half * W, half * W + W
        e, g = ext[1][s], grad[1][s]
        out[s, :, a:b, 0:W] = e[:, 0, a:b, :] - STEP * (g[:, 0, a:b, :] + cleft[1][s][:, a:b, :])
        out[s, :, a:b, W:] = e[:, 1, a:b, :] - STEP * g[:, 1, a:b, :]

    corner(0)
    phase_a(ext[0][0])
    corner(1)
    phase_b(ext[0][1], grad[0][1])
    f1, h1 = fold_start(0, 1)
    phase_c(grad[0][0])
    l1 = fold_next(0, 1, f1)
    f0, h0 = fold_start(0, 0)
    l0 = fold_next(0, 0, f0)
    for s, lows, highs in ((1, l1, h1), (0, l0, h0)):
        update(s, 0, lows)
        n = ext[1][s]
        halo[s] = send(n.at[:, :, lo], n.at[:, :, over], up)
        update(s, 1, highs)

    halo[0].wait_recv()
    phase_a(ext[1][0])
    halo[1].wait_recv()
    phase_b(ext[1][1], grad[1][1])
    f1, h1 = fold_start(1, 1)
    phase_c(grad[1][0])
    l1 = fold_next(1, 1, f1)
    f0, h0 = fold_start(1, 0)
    l0 = fold_next(1, 0, f0)
    for s, lows, highs in ((1, l1, h1), (0, l0, h0)):
        finish(s, 0, lows)
        finish(s, 1, highs)
    for c in started:
        c.wait_send()


COPIES = 40


def body(specimen, probe, phase, amplitudes, positions, counts, order):
    th, tl = tables()
    ext = pltpu.VMEM((2, 3, TILE + W, W), F32)
    rfold = pltpu.VMEM((2, 3, W, W), F32)
    strip = pltpu.VMEM((2, TILE, W), F32)
    wave = pltpu.VMEM((2, 2 * W, 2 * W), F32)
    vmem = pl.BlockSpec(memory_space=pltpu.VMEM)
    smem = pl.BlockSpec(memory_space=pltpu.SMEM)
    return pl.pallas_call(
        kernel,
        out_shape=jax.ShapeDtypeStruct(specimen.shape, F32),
        in_specs=[smem] * 3 + [vmem] * 6,
        out_specs=vmem,
        scratch_shapes=[ext] * 8 + [rfold] * 4 + [strip] * 6
        + [
            pltpu.VMEM((SLOTS, 2, 3, 2 * TILE + W, W), F32),
            pltpu.VMEM((2 * W, 2 * W), F32),
            pltpu.VMEM((2 * W, 2 * W), F32),
            wave, wave, wave,
            pltpu.SemaphoreType.DMA((COPIES,)),
            pltpu.SemaphoreType.DMA((COPIES,)),
        ],
        compiler_params=pltpu.CompilerParams(
            collective_id=0, has_side_effects=True, vmem_limit_bytes=56 * 2**20
        ),
    )(
        positions[0, 0], counts[0], order[0, 0],
        specimen, probe, phase, amplitudes[0, 0], th, tl,
    )


def solution(mesh):
    placed = (
        P(None, None, "row", "col"),
        P(),
        P(),
        P("row", "col", None, None, None),
        P("row", "col", None, None),
        P("row", "col"),
        P("row", "col", None),
    )
    return jax.shard_map(
        body, mesh=mesh, in_specs=placed, out_specs=P(None, None, "row", "col"), check_vma=False
    )
```

```python
import math

import jax
import jax.numpy as jnp
import numpy as np
from jax import lax
from jax.experimental import pallas as pl
from jax.experimental.pallas import tpu as pltpu
from jax.sharding import PartitionSpec as P

SLOTS = 4
RUN = 8
W = 128
TILE = 256
STEP = 0.02
FLOOR = 0.5
F32 = jnp.float32
BF16 = jnp.bfloat16
MESH = pl.DeviceIdType.MESH


def tables():
    k = np.arange(W)
    angle = (k[:, None] * k[None, :] % W) * (2.0 * math.pi / W)
    re = np.cos(angle) / math.sqrt(W)
    im = -np.sin(angle) / math.sqrt(W)
    forward = np.block([[re, im], [-im, re]]).astype(np.float32)
    backward = np.block([[re, -im], [im, re]]).astype(np.float32)
    both = jnp.asarray(np.stack([forward, backward]))
    high = both.astype(BF16)
    low = (both - high.astype(F32)).astype(BF16)
    return high, low


def split(v):
    high = v.astype(BF16)
    return high, (v - high.astype(F32)).astype(BF16)


def dot(a, b):
    return jnp.dot(a, b, preferred_element_type=F32)


def swap_blocks(v):
    top = jnp.concatenate([v[:W, :W], v[W:, :W]], 1)
    bottom = jnp.concatenate([v[:W, W:], v[W:, W:]], 1)
    return jnp.concatenate([top, bottom], 0)


def transform(v, left, right):
    vh, vl = split(v)
    v = dot(left[0], vh) + (dot(left[1], vh) + dot(left[0], vl))
    vh, vl = split(swap_blocks(v))
    v = dot(vh, right[0]) + (dot(vh, right[1]) + dot(vl, right[0]))
    return swap_blocks(v)


def cmul(a, b):
    ar, ai, br, bi = a[:W], a[W:], b[:W], b[W:]
    return jnp.concatenate([ar * br - ai * bi, ar * bi + ai * br], 0)


def cmul_conj(a, b):
    ar, ai, br, bi = a[:W], a[W:], b[:W], b[W:]
    return jnp.concatenate([ar * br + ai * bi, ar * bi - ai * br], 0)


def kernel(
    pos, cnt, order,
    x, probe_in, phase, amp, th, tl,
    out,
    ea0, ea1, eb0, eb1, ga0, ga1, gb0, gb1,
    rfa0, rfa1, rfb0, rfb1, upa0, upa1, upb0, upb1, cla0, cla1, clb0, clb1, cr0, cr1,
    pad, prb, prp, q_s, o2_s, back_s,
    ssem, rsem, vsem,
):
    row, col = lax.axis_index("row"), lax.axis_index("col")
    n_row, n_col = lax.axis_size("row"), lax.axis_size("col")
    spot = lax.rem(row, RUN)

    def at_row(distance):
        return (lax.rem(row + n_row + distance, n_row), col)

    left = (row, lax.rem(col + n_col - 1, n_col))
    right = (row, lax.rem(col + 1, n_col))
    ext = ((ea0, ea1), (eb0, eb1))
    grad = ((ga0, ga1), (gb0, gb1))
    rfold = ((rfa0, rfa1), (rfb0, rfb1))
    above = ((upa0, upa1), (upb0, upb1))
    cleft = ((cla0, cla1), (clb0, clb1))
    cright = (cr0, cr1)
    taken = [0]
    started = []

    def send(src, dst, device):
        i = taken[0]
        taken[0] += 1
        copy = pltpu.make_async_remote_copy(
            src_ref=src, dst_ref=dst, send_sem=ssem.at[i], recv_sem=rsem.at[i],
            device_id=device, device_id_type=MESH,
        )
        copy.start()
        started.append(copy)
        return copy

    def strip(ways, land, way, turn, blocks):
        base = ways[0]
        ends = spot == turn
        for b, src in blocks:
            far = ends if b else False
            i = taken[0]
            taken[0] += 1
            hops = jnp.where(far, -2 * b * way, way)
            copy = pltpu.make_async_remote_copy(
                src_ref=src, dst_ref=land.at[jnp.where(far, 1, 0), b],
                send_sem=ssem.at[i],
                recv_sem=vsem.at[jnp.where(far, 1, 0), base + b],
                device_id=at_row(hops), device_id_type=MESH,
            )
            copy.start()
            started.append(copy)

    def hop(ways, land, way, turn):
        base, k = ways
        for b in (1, 2):
            @pl.when(spot == turn - 2 * b * way)
            def _():
                copy = pltpu.make_async_remote_copy(
                    src_ref=land.at[1, b], dst_ref=land.at[1, b],
                    send_sem=vsem.at[2, k], recv_sem=vsem.at[1, base + b],
                    device_id=at_row((2 * b + 1) * way), device_id_type=MESH,
                )
                copy.wait_recv()
                pltpu.make_async_remote_copy(
                    src_ref=land.at[1, b], dst_ref=land.at[0, b],
                    send_sem=vsem.at[2, k], recv_sem=vsem.at[0, base + b],
                    device_id=at_row((2 * b + 1) * way), device_id_type=MESH,
                ).start()
        hops_made.append((ways, land, way, turn))

    def hop_end(ways, land, way, turn):
        base, k = ways
        for b in (1, 2):
            @pl.when(spot == turn - 2 * b * way)
            def _():
                pltpu.make_async_remote_copy(
                    src_ref=land.at[1, b], dst_ref=land.at[0, b],
                    send_sem=vsem.at[2, k], recv_sem=vsem.at[0, base + b],
                    device_id=at_row((2 * b + 1) * way), device_id_type=MESH,
                ).wait_send()

    def landed(ways, land, blocks):
        for b in blocks:
            pltpu.make_async_remote_copy(
                src_ref=land.at[0, b], dst_ref=land.at[0, b],
                send_sem=vsem.at[2, ways[1]], recv_sem=vsem.at[0, ways[0] + b],
                device_id=at_row(1), device_id_type=MESH,
            ).wait_recv()

    hops_made = []
    UP, DOWN = (-1, 0), (1, RUN - 1)

    def ways_of(kind, t, s):
        k = (kind * 2 + t) * 2 + s
        return 3 * k, k

    barrier = pltpu.get_barrier_semaphore()
    near = [at_row(d * k) for k in range(1, 6) for d in (-1, 1)]
    for d in near + [left, right]:
        pl.semaphore_signal(barrier, inc=1, device_id=d, device_id_type=MESH)
    pl.semaphore_wait(barrier, len(near) + 2)

    lo, hi, all_rows, over = pl.ds(0, W), pl.ds(W, W), pl.ds(0, TILE), pl.ds(TILE, W)

    halo = []
    for s in range(2):
        e = ext[0][s]
        c0 = send(x.at[s, :, lo, lo], e.at[:, 2, lo], left)
        strip(ways_of(0, 0, s), above[0][s], *UP, ((0, x.at[s, :, lo, lo]), (1, x.at[s, :, lo, hi])))
        c1 = send(x.at[s, :, hi, lo], e.at[:, 2, hi], left)
        halo.append((c0, c1))

    for s in range(2):
        for b in range(2):
            ext[0][s][:, b, 0:TILE, :] = x[s, :, :, b * W:(b + 1) * W]
    pad[:, :, :, 0:TILE, :] = jnp.zeros((SLOTS, 2, 3, TILE, W), F32)
    pad[:, :, :, TILE + W:, :] = jnp.zeros((SLOTS, 2, 3, TILE, W), F32)
    for i in range(2):
        p = probe_in[i]
        prb[i * W:(i + 1) * W, :] = jnp.concatenate([p, p], 1)
    cs, sn = jnp.cos(phase[...]), jnp.sin(phase[...])
    prp[0:W, :] = jnp.concatenate([cs, cs], 1)
    prp[W:, :] = jnp.concatenate([sn, sn], 1)

    def corner(s):
        halo[s][0].wait_recv()
        strip(ways_of(0, 0, s), above[0][s], *UP, ((2, ext[0][s].at[:, 2, lo]),))

    def extend(t, s):
        ways = ways_of(0, t, s)
        landed(ways, above[t][s], range(3))
        for b in range(3):
            ext[t][s][:, b, TILE:, :] = above[t][s][0, b]

    def hop_up(t, s):
        hop(ways_of(0, t, s), above[t][s], *UP)

    def hop_down(t, s):
        hop(ways_of(1, t, s), rfold[t][s], *DOWN)

    lane = lax.broadcasted_iota(jnp.int32, (W, W), 1)

    def place(j):
        r, c = pos[0, j], pos[1, j]
        h = lax.shift_right_logical(c, 7)
        return r, h, c - h * W

    def window(e, j):
        r, h, s = place(j)
        back = lax.rem(W - s, W)
        parts = []
        for i in range(2):
            a = pltpu.roll(e[i, h, pl.ds(r, W), :], back, 1)
            b = pltpu.roll(e[i, h + 1, pl.ds(r, W), :], back, 1)
            parts.append(jnp.where(lane < W - s, a, b))
        return jnp.concatenate(parts, 0)

    def pair_window(e, p):
        return jnp.concatenate([window(e, 2 * p), window(e, 2 * p + 1)], 1)

    def spread(g, p):
        for k in range(2):
            j = 2 * p + k
            r, h, s = place(j)
            live = j < cnt[0]
            for i in range(2):
                v = pltpu.roll(g[i * W:(i + 1) * W, k * W:(k + 1) * W], s, 1)
                v = jnp.where(live, v, 0.0)
                first = jnp.where(lane >= s, v, 0.0)
                second = jnp.where(lane >= s, 0.0, v)
                pad[j, i, 0, over, :] = jnp.where(h == 0, first, 0.0)
                pad[j, i, 1, over, :] = jnp.where(h == 0, second, first)
                pad[j, i, 2, over, :] = jnp.where(h == 0, 0.0, second)

    def collect(g):
        starts = [TILE - place(j)[0] for j in range(SLOTS)]
        for i in range(2):
            for b in range(3):
                v = pad[0, i, b, pl.ds(starts[0], TILE + W), :]
                for j in range(1, SLOTS):
                    v = v + pad[j, i, b, pl.ds(starts[j], TILE + W), :]
                g[i, b] = v

    def fwd(v):
        return transform(v, (th[1], tl[1]), (th[0], tl[0]))

    def bwd(v):
        return transform(v, (th[0], tl[0]), (th[1], tl[1]))

    def phase_a(e):
        for p in range(2):
            v = fwd(cmul(prb[...], pair_window(e, p)))
            q_s[p] = bwd(cmul(prp[...], v))

    def phase_b(e, g):
        for p in range(2):
            o2 = pair_window(e, p)
            o2_s[p] = o2
            psi = fwd(cmul(q_s[p], o2))
            pr, pi = psi[:W], psi[W:]
            m = jnp.concatenate([amp[order[2 * p]], amp[order[2 * p + 1]]], 1)
            f = 1.0 - m / jnp.maximum(jnp.sqrt(pr * pr + pi * pi), FLOOR)
            d2 = bwd(jnp.concatenate([pr * f, pi * f], 0))
            spread(cmul_conj(q_s[p], d2), p)
            back_s[p] = cmul_conj(o2_s[p], d2)
        collect(g)

    def phase_c(g):
        for p in range(2):
            v = bwd(cmul_conj(prp[...], fwd(back_s[p])))
            spread(cmul_conj(prb[...], v), p)
        collect(g)

    def fold_start(t, s):
        g = grad[t][s]
        strip(ways_of(1, t, s), rfold[t][s], *DOWN, [(b, g.at[:, b, over]) for b in range(3)])

    def trade(t, s, rows):
        g = grad[t][s]
        cs = [send(g.at[:, 2, rows], cleft[t][s].at[:, rows], right)]
        if t == 0:
            cs.append(send(g.at[:, 0, rows], cright[s].at[:, rows], left))
        return cs

    def fold_end(t, s):
        g = grad[t][s]
        landed(ways_of(1, t, s), rfold[t][s], range(3))
        for b in range(3):
            g[:, b, 0:W, :] += rfold[t][s][0, b]

    def update(s, half, cs):
        for c in cs:
            c.wait_recv()
        a, b = half * W, half * W + W
        e, g, n = ext[0][s], grad[0][s], ext[1][s]
        n[:, 0, a:b, :] = e[:, 0, a:b, :] - STEP * (g[:, 0, a:b, :] + cleft[0][s][:, a:b, :])
        n[:, 1, a:b, :] = e[:, 1, a:b, :] - STEP * g[:, 1, a:b, :]
        n[:, 2, a:b, :] = e[:, 2, a:b, :] - STEP * (g[:, 2, a:b, :] + cright[s][:, a:b, :])

    def finish(s, half, cs):
        for c in cs:
            c.wait_recv()
        a, b = half * W, half * W + W
        e, g = ext[1][s], grad[1][s]
        out[s, :, a:b, 0:W] = e[:, 0, a:b, :] - STEP * (g[:, 0, a:b, :] + cleft[1][s][:, a:b, :])
        out[s, :, a:b, W:] = e[:, 1, a:b, :] - STEP * g[:, 1, a:b, :]

    corner(0)
    hop_up(0, 0)
    corner(1)
    hop_up(0, 1)
    halo[0][1].wait_recv()
    extend(0, 0)
    phase_a(ext[0][0])
    halo[1][1].wait_recv()
    extend(0, 1)
    phase_b(ext[0][1], grad[0][1])
    fold_start(0, 1)
    h1 = trade(0, 1, hi)
    phase_c(grad[0][0])
    fold_start(0, 0)
    hop_down(0, 1)
    hop_down(0, 0)
    fold_end(0, 1)
    l1 = trade(0, 1, lo)
    fold_end(0, 0)
    l0 = trade(0, 0, lo)
    h0 = trade(0, 0, hi)
    for s, lows in ((1, l1), (0, l0)):
        update(s, 0, lows)
        strip(ways_of(0, 1, s), above[1][s], *UP, [(b, ext[1][s].at[:, b, lo]) for b in range(3)])
    hop_up(1, 1)
    hop_up(1, 0)
    update(1, 1, h1)
    update(0, 1, h0)

    extend(1, 0)
    phase_a(ext[1][0])
    extend(1, 1)
    phase_b(ext[1][1], grad[1][1])
    fold_start(1, 1)
    h1 = trade(1, 1, hi)
    phase_c(grad[1][0])
    fold_start(1, 0)
    h0 = trade(1, 0, hi)
    hop_down(1, 1)
    hop_down(1, 0)
    fold_end(1, 1)
    l1 = trade(1, 1, lo)
    fold_end(1, 0)
    l0 = trade(1, 0, lo)
    finish(1, 1, h1)
    finish(0, 1, h0)
    finish(1, 0, l1)
    finish(0, 0, l0)
    for c in started:
        c.wait_send()
    for h in hops_made:
        hop_end(*h)


COPIES = 60


def body(specimen, probe, phase, amplitudes, positions, counts, order):
    th, tl = tables()
    ext = pltpu.VMEM((2, 3, TILE + W, W), F32)
    edge = pltpu.VMEM((2, 3, 2, W, W), F32)
    strip = pltpu.VMEM((2, TILE, W), F32)
    wave = pltpu.VMEM((2, 2 * W, 2 * W), F32)
    vmem = pl.BlockSpec(memory_space=pltpu.VMEM)
    smem = pl.BlockSpec(memory_space=pltpu.SMEM)
    return pl.pallas_call(
        kernel,
        out_shape=jax.ShapeDtypeStruct(specimen.shape, F32),
        in_specs=[smem] * 3 + [vmem] * 6,
        out_specs=vmem,
        scratch_shapes=[ext] * 8 + [edge] * 8 + [strip] * 6
        + [
            pltpu.VMEM((SLOTS, 2, 3, 2 * TILE + W, W), F32),
            pltpu.VMEM((2 * W, 2 * W), F32),
            pltpu.VMEM((2 * W, 2 * W), F32),
            wave, wave, wave,
            pltpu.SemaphoreType.DMA((COPIES,)),
            pltpu.SemaphoreType.DMA((COPIES,)),
            pltpu.SemaphoreType.DMA((3, 24)),
        ],
        compiler_params=pltpu.CompilerParams(
            collective_id=0, has_side_effects=True, vmem_limit_bytes=56 * 2**20
        ),
    )(
        positions[0, 0].T, counts[0], order[0, 0],
        specimen, probe, phase, amplitudes[0, 0], th, tl,
    )


def solution(mesh):
    placed = (
        P(None, None, "row", "col"),
        P(),
        P(),
        P("row", "col", None, None, None),
        P("row", "col", None, None),
        P("row", "col"),
        P("row", "col", None),
    )
    return jax.shard_map(
        body, mesh=mesh, in_specs=placed, out_specs=P(None, None, "row", "col"), check_vma=False
    )
```

```python
import math

import jax
import jax.numpy as jnp
import numpy as np
from jax import lax
from jax.experimental import pallas as pl
from jax.experimental.pallas import tpu as pltpu
from jax.sharding import PartitionSpec as P

SLOTS = 4
RUN = 8
W = 128
TILE = 256
STEP = 0.02
FLOOR = 0.5
F32 = jnp.float32
BF16 = jnp.bfloat16
MESH = pl.DeviceIdType.MESH


def tables():
    k = np.arange(W)
    angle = (k[:, None] * k[None, :] % W) * (2.0 * math.pi / W)
    re = np.cos(angle) / math.sqrt(W)
    im = -np.sin(angle) / math.sqrt(W)
    forward = np.block([[re, im], [-im, re]]).astype(np.float32)
    backward = np.block([[re, -im], [im, re]]).astype(np.float32)
    both = jnp.asarray(np.stack([forward, backward]))
    high = both.astype(BF16)
    low = (both - high.astype(F32)).astype(BF16)
    return high, low


def split(v):
    high = v.astype(BF16)
    return high, (v - high.astype(F32)).astype(BF16)


def dot(a, b):
    return jnp.dot(a, b, preferred_element_type=F32)


def swap_blocks(v):
    top = jnp.concatenate([v[:W, :W], v[W:, :W]], 1)
    bottom = jnp.concatenate([v[:W, W:], v[W:, W:]], 1)
    return jnp.concatenate([top, bottom], 0)


def transform(v, left, right):
    vh, vl = split(v)
    v = dot(left[0], vh) + (dot(left[1], vh) + dot(left[0], vl))
    vh, vl = split(swap_blocks(v))
    v = dot(vh, right[0]) + (dot(vh, right[1]) + dot(vl, right[0]))
    return swap_blocks(v)


def cmul(a, b):
    ar, ai, br, bi = a[:W], a[W:], b[:W], b[W:]
    return jnp.concatenate([ar * br - ai * bi, ar * bi + ai * br], 0)


def cmul_conj(a, b):
    ar, ai, br, bi = a[:W], a[W:], b[:W], b[W:]
    return jnp.concatenate([ar * br + ai * bi, ar * bi - ai * br], 0)


def kernel(
    pos, cnt, order,
    x, probe_in, phase, amp, th, tl,
    out,
    ea0, ea1, eb0, eb1, ga0, ga1, gb0, gb1,
    rfa0, rfa1, rfb0, rfb1, upa0, upa1, upb0, upb1, cla0, cla1, clb0, clb1, cr0, cr1,
    pad, prb, prp, q_s, o2_s, back_s,
    ssem, rsem, vsem,
):
    row, col = lax.axis_index("row"), lax.axis_index("col")
    n_row, n_col = lax.axis_size("row"), lax.axis_size("col")
    spot = lax.rem(row, RUN)

    def at_row(distance):
        return (lax.rem(row + n_row + distance, n_row), col)

    left = (row, lax.rem(col + n_col - 1, n_col))
    right = (row, lax.rem(col + 1, n_col))
    ext = ((ea0, ea1), (eb0, eb1))
    grad = ((ga0, ga1), (gb0, gb1))
    rfold = ((rfa0, rfa1), (rfb0, rfb1))
    above = ((upa0, upa1), (upb0, upb1))
    cleft = ((cla0, cla1), (clb0, clb1))
    cright = (cr0, cr1)
    taken = [0]
    started = []

    def send(src, dst, device):
        i = taken[0]
        taken[0] += 1
        copy = pltpu.make_async_remote_copy(
            src_ref=src, dst_ref=dst, send_sem=ssem.at[i], recv_sem=rsem.at[i],
            device_id=device, device_id_type=MESH,
        )
        copy.start()
        started.append(copy)
        return copy

    def strip(ways, land, way, turn, blocks):
        base = ways[0]
        ends = spot == turn
        for b, src in blocks:
            far = ends if b else False
            i = taken[0]
            taken[0] += 1
            hops = jnp.where(far, -2 * b * way, way)
            copy = pltpu.make_async_remote_copy(
                src_ref=src, dst_ref=land.at[jnp.where(far, 1, 0), b],
                send_sem=ssem.at[i],
                recv_sem=vsem.at[jnp.where(far, 1, 0), base + b],
                device_id=at_row(hops), device_id_type=MESH,
            )
            copy.start()
            started.append(copy)

    def hop(ways, land, way, turn):
        base, k = ways
        for b in (1, 2):
            @pl.when(spot == turn - 2 * b * way)
            def _():
                copy = pltpu.make_async_remote_copy(
                    src_ref=land.at[1, b], dst_ref=land.at[1, b],
                    send_sem=vsem.at[2, k], recv_sem=vsem.at[1, base + b],
                    device_id=at_row((2 * b + 1) * way), device_id_type=MESH,
                )
                copy.wait_recv()
                pltpu.make_async_remote_copy(
                    src_ref=land.at[1, b], dst_ref=land.at[0, b],
                    send_sem=vsem.at[2, k], recv_sem=vsem.at[0, base + b],
                    device_id=at_row((2 * b + 1) * way), device_id_type=MESH,
                ).start()
        hops_made.append((ways, land, way, turn))

    def hop_end(ways, land, way, turn):
        base, k = ways
        for b in (1, 2):
            @pl.when(spot == turn - 2 * b * way)
            def _():
                pltpu.make_async_remote_copy(
                    src_ref=land.at[1, b], dst_ref=land.at[0, b],
                    send_sem=vsem.at[2, k], recv_sem=vsem.at[0, base + b],
                    device_id=at_row((2 * b + 1) * way), device_id_type=MESH,
                ).wait_send()

    def landed(ways, land, blocks):
        for b in blocks:
            pltpu.make_async_remote_copy(
                src_ref=land.at[0, b], dst_ref=land.at[0, b],
                send_sem=vsem.at[2, ways[1]], recv_sem=vsem.at[0, ways[0] + b],
                device_id=at_row(1), device_id_type=MESH,
            ).wait_recv()

    hops_made = []
    UP, DOWN = (-1, 0), (1, RUN - 1)

    def ways_of(kind, t, s):
        k = (kind * 2 + t) * 2 + s
        return 3 * k, k

    barrier = pltpu.get_barrier_semaphore()
    near = [at_row(d * k) for k in range(1, 6) for d in (-1, 1)]
    for d in near + [left, right]:
        pl.semaphore_signal(barrier, inc=1, device_id=d, device_id_type=MESH)
    pl.semaphore_wait(barrier, len(near) + 2)

    lo, hi, all_rows, over = pl.ds(0, W), pl.ds(W, W), pl.ds(0, TILE), pl.ds(TILE, W)

    halo = []
    for s in range(2):
        e = ext[0][s]
        c0 = send(x.at[s, :, lo, lo], e.at[:, 2, lo], left)
        halo.append(c0)
        strip(ways_of(0, 0, s), above[0][s], *UP, ((0, x.at[s, :, lo, lo]), (1, x.at[s, :, lo, hi])))

    rest = [send(x.at[s, :, hi, lo], ext[0][s].at[:, 2, hi], left) for s in range(2)]

    for s in range(2):
        for b in range(2):
            ext[0][s][:, b, 0:TILE, :] = x[s, :, :, b * W:(b + 1) * W]
    pad[:, :, :, 0:TILE, :] = jnp.zeros((SLOTS, 2, 3, TILE, W), F32)
    pad[:, :, :, TILE + W:, :] = jnp.zeros((SLOTS, 2, 3, TILE, W), F32)
    for i in range(2):
        p = probe_in[i]
        prb[i * W:(i + 1) * W, :] = jnp.concatenate([p, p], 1)
    cs, sn = jnp.cos(phase[...]), jnp.sin(phase[...])
    prp[0:W, :] = jnp.concatenate([cs, cs], 1)
    prp[W:, :] = jnp.concatenate([sn, sn], 1)

    def corner(s):
        halo[s].wait_recv()
        strip(ways_of(0, 0, s), above[0][s], *UP, ((2, ext[0][s].at[:, 2, lo]),))

    def extend(t, s):
        ways = ways_of(0, t, s)
        landed(ways, above[t][s], range(3))
        for b in range(3):
            ext[t][s][:, b, TILE:, :] = above[t][s][0, b]

    def hop_up(t, s):
        hop(ways_of(0, t, s), above[t][s], *UP)

    def hop_down(t, s):
        hop(ways_of(1, t, s), rfold[t][s], *DOWN)

    lane = lax.broadcasted_iota(jnp.int32, (W, W), 1)

    def place(j):
        r, c = pos[0, j], pos[1, j]
        h = lax.shift_right_logical(c, 7)
        return r, h, c - h * W

    def window(e, j):
        r, h, s = place(j)
        back = lax.rem(W - s, W)
        parts = []
        for i in range(2):
            a = pltpu.roll(e[i, h, pl.ds(r, W), :], back, 1)
            b = pltpu.roll(e[i, h + 1, pl.ds(r, W), :], back, 1)
            parts.append(jnp.where(lane < W - s, a, b))
        return jnp.concatenate(parts, 0)

    def pair_window(e, p):
        return jnp.concatenate([window(e, 2 * p), window(e, 2 * p + 1)], 1)

    def spread(g, p):
        for k in range(2):
            j = 2 * p + k
            r, h, s = place(j)
            live = j < cnt[0]
            for i in range(2):
                v = pltpu.roll(g[i * W:(i + 1) * W, k * W:(k + 1) * W], s, 1)
                v = jnp.where(live, v, 0.0)
                first = jnp.where(lane >= s, v, 0.0)
                second = jnp.where(lane >= s, 0.0, v)
                pad[j, i, 0, over, :] = jnp.where(h == 0, first, 0.0)
                pad[j, i, 1, over, :] = jnp.where(h == 0, second, first)
                pad[j, i, 2, over, :] = jnp.where(h == 0, 0.0, second)

    def collect(g):
        starts = [TILE - place(j)[0] for j in range(SLOTS)]
        for i in range(2):
            for b in range(3):
                v = pad[0, i, b, pl.ds(starts[0], TILE + W), :]
                for j in range(1, SLOTS):
                    v = v + pad[j, i, b, pl.ds(starts[j], TILE + W), :]
                g[i, b] = v

    def fwd(v):
        return transform(v, (th[1], tl[1]), (th[0], tl[0]))

    def bwd(v):
        return transform(v, (th[0], tl[0]), (th[1], tl[1]))

    def phase_a(e):
        for p in range(2):
            v = fwd(cmul(prb[...], pair_window(e, p)))
            q_s[p] = bwd(cmul(prp[...], v))

    def phase_b(e, g):
        for p in range(2):
            o2 = pair_window(e, p)
            o2_s[p] = o2
            psi = fwd(cmul(q_s[p], o2))
            pr, pi = psi[:W], psi[W:]
            m = jnp.concatenate([amp[order[2 * p]], amp[order[2 * p + 1]]], 1)
            f = 1.0 - m / jnp.maximum(jnp.sqrt(pr * pr + pi * pi), FLOOR)
            d2 = bwd(jnp.concatenate([pr * f, pi * f], 0))
            spread(cmul_conj(q_s[p], d2), p)
            back_s[p] = cmul_conj(o2_s[p], d2)
        collect(g)

    def phase_c(g):
        for p in range(2):
            v = bwd(cmul_conj(prp[...], fwd(back_s[p])))
            spread(cmul_conj(prb[...], v), p)
        collect(g)

    def fold_start(t, s):
        g = grad[t][s]
        strip(ways_of(1, t, s), rfold[t][s], *DOWN, [(b, g.at[:, b, over]) for b in range(3)])

    def trade(t, s, rows):
        g = grad[t][s]
        cs = [send(g.at[:, 2, rows], cleft[t][s].at[:, rows], right)]
        if t == 0:
            cs.append(send(g.at[:, 0, rows], cright[s].at[:, rows], left))
        return cs

    def fold_end(t, s):
        g = grad[t][s]
        landed(ways_of(1, t, s), rfold[t][s], range(3))
        for b in range(3):
            g[:, b, 0:W, :] += rfold[t][s][0, b]

    def update(s, half, cs):
        for c in cs:
            c.wait_recv()
        a, b = half * W, half * W + W
        e, g, n = ext[0][s], grad[0][s], ext[1][s]
        n[:, 0, a:b, :] = e[:, 0, a:b, :] - STEP * (g[:, 0, a:b, :] + cleft[0][s][:, a:b, :])
        n[:, 1, a:b, :] = e[:, 1, a:b, :] - STEP * g[:, 1, a:b, :]
        n[:, 2, a:b, :] = e[:, 2, a:b, :] - STEP * (g[:, 2, a:b, :] + cright[s][:, a:b, :])

    def finish(s, half, cs):
        for c in cs:
            c.wait_recv()
        a, b = half * W, half * W + W
        e, g = ext[1][s], grad[1][s]
        out[s, :, a:b, 0:W] = e[:, 0, a:b, :] - STEP * (g[:, 0, a:b, :] + cleft[1][s][:, a:b, :])
        out[s, :, a:b, W:] = e[:, 1, a:b, :] - STEP * g[:, 1, a:b, :]

    def lower(s, lows):
        update(s, 0, lows)
        strip(ways_of(0, 1, s), above[1][s], *UP, [(b, ext[1][s].at[:, b, lo]) for b in range(3)])

    corner(0)
    corner(1)
    hop_up(0, 0)
    hop_up(0, 1)
    rest[0].wait_recv()
    extend(0, 0)
    phase_a(ext[0][0])
    rest[1].wait_recv()
    extend(0, 1)
    phase_b(ext[0][1], grad[0][1])
    fold_start(0, 1)
    h1 = trade(0, 1, pl.ds(W, W // 2))
    phase_c(grad[0][0])
    fold_start(0, 0)
    hop_down(0, 1)
    hop_down(0, 0)
    fold_end(0, 0)
    l0 = trade(0, 0, lo)
    fold_end(0, 1)
    l1 = trade(0, 1, lo)
    h0 = trade(0, 0, hi)
    k1 = trade(0, 1, pl.ds(W + W // 2, W // 2))
    lower(0, l0)
    lower(1, l1)
    hop_up(1, 0)
    hop_up(1, 1)
    update(0, 1, h0)
    extend(1, 0)
    phase_a(ext[1][0])
    update(1, 1, h1 + k1)
    extend(1, 1)
    phase_b(ext[1][1], grad[1][1])
    fold_start(1, 1)
    h1 = trade(1, 1, hi)
    phase_c(grad[1][0])
    fold_start(1, 0)
    h0 = trade(1, 0, hi)
    hop_down(1, 1)
    hop_down(1, 0)
    fold_end(1, 1)
    l1 = trade(1, 1, lo)
    fold_end(1, 0)
    l0 = trade(1, 0, lo)
    finish(1, 1, h1)
    finish(0, 1, h0)
    finish(1, 0, l1)
    finish(0, 0, l0)
    for c in started:
        c.wait_send()
    for h in hops_made:
        hop_end(*h)


COPIES = 60


def body(specimen, probe, phase, amplitudes, positions, counts, order):
    th, tl = tables()
    ext = pltpu.VMEM((2, 3, TILE + W, W), F32)
    edge = pltpu.VMEM((2, 3, 2, W, W), F32)
    strip = pltpu.VMEM((2, TILE, W), F32)
    wave = pltpu.VMEM((2, 2 * W, 2 * W), F32)
    vmem = pl.BlockSpec(memory_space=pltpu.VMEM)
    smem = pl.BlockSpec(memory_space=pltpu.SMEM)
    return pl.pallas_call(
        kernel,
        out_shape=jax.ShapeDtypeStruct(specimen.shape, F32),
        in_specs=[smem] * 3 + [vmem] * 6,
        out_specs=vmem,
        scratch_shapes=[ext] * 8 + [edge] * 8 + [strip] * 6
        + [
            pltpu.VMEM((SLOTS, 2, 3, 2 * TILE + W, W), F32),
            pltpu.VMEM((2 * W, 2 * W), F32),
            pltpu.VMEM((2 * W, 2 * W), F32),
            wave, wave, wave,
            pltpu.SemaphoreType.DMA((COPIES,)),
            pltpu.SemaphoreType.DMA((COPIES,)),
            pltpu.SemaphoreType.DMA((3, 24)),
        ],
        compiler_params=pltpu.CompilerParams(
            collective_id=0, has_side_effects=True, vmem_limit_bytes=56 * 2**20
        ),
    )(
        positions[0, 0].T, counts[0], order[0, 0],
        specimen, probe, phase, amplitudes[0, 0], th, tl,
    )


def solution(mesh):
    placed = (
        P(None, None, "row", "col"),
        P(),
        P(),
        P("row", "col", None, None, None),
        P("row", "col", None, None),
        P("row", "col"),
        P("row", "col", None),
    )
    return jax.shard_map(
        body, mesh=mesh, in_specs=placed, out_specs=P(None, None, "row", "col"), check_vma=False
    )
```

```python
import math

import jax
import jax.numpy as jnp
import numpy as np
from jax import lax
from jax.experimental import pallas as pl
from jax.experimental.pallas import tpu as pltpu
from jax.sharding import PartitionSpec as P

SLOTS = 4
RUN = 8
W = 128
TILE = 256
STEP = 0.02
FLOOR = 0.5
F32 = jnp.float32
BF16 = jnp.bfloat16
MESH = pl.DeviceIdType.MESH


def tables():
    k = np.arange(W)
    angle = (k[:, None] * k[None, :] % W) * (2.0 * math.pi / W)
    re = np.cos(angle) / math.sqrt(W)
    im = -np.sin(angle) / math.sqrt(W)
    forward = np.block([[re, im], [-im, re]]).astype(np.float32)
    backward = np.block([[re, -im], [im, re]]).astype(np.float32)
    both = jnp.asarray(np.stack([forward, backward]))
    high = both.astype(BF16)
    low = (both - high.astype(F32)).astype(BF16)
    return high, low


def split(v):
    high = v.astype(BF16)
    return high, (v - high.astype(F32)).astype(BF16)


def dot(a, b):
    return jnp.dot(a, b, preferred_element_type=F32)


def swap_blocks(v):
    top = jnp.concatenate([v[:W, :W], v[W:, :W]], 1)
    bottom = jnp.concatenate([v[:W, W:], v[W:, W:]], 1)
    return jnp.concatenate([top, bottom], 0)


def transform(v, left, right):
    vh, vl = split(v)
    v = dot(left[0], vh) + (dot(left[1], vh) + dot(left[0], vl))
    vh, vl = split(swap_blocks(v))
    v = dot(vh, right[0]) + (dot(vh, right[1]) + dot(vl, right[0]))
    return swap_blocks(v)


def cmul(a, b):
    ar, ai, br, bi = a[:W], a[W:], b[:W], b[W:]
    return jnp.concatenate([ar * br - ai * bi, ar * bi + ai * br], 0)


def cmul_conj(a, b):
    ar, ai, br, bi = a[:W], a[W:], b[:W], b[W:]
    return jnp.concatenate([ar * br + ai * bi, ar * bi - ai * br], 0)


def kernel(
    pos, cnt, order,
    x, probe_in, phase, amp, th, tl,
    out,
    ea0, ea1, eb0, eb1, ga0, ga1, gb0, gb1,
    rfa0, rfa1, rfb0, rfb1, upa0, upa1, upb0, upb1, cla0, cla1, clb0, clb1, cr0, cr1,
    pad, prb, prp, q_s, o2_s, back_s,
    ssem, rsem, vsem,
):
    row, col = lax.axis_index("row"), lax.axis_index("col")
    n_row, n_col = lax.axis_size("row"), lax.axis_size("col")
    spot = lax.rem(row, RUN)

    def at_row(distance):
        return (lax.rem(row + n_row + distance, n_row), col)

    left = (row, lax.rem(col + n_col - 1, n_col))
    right = (row, lax.rem(col + 1, n_col))
    ext = ((ea0, ea1), (eb0, eb1))
    grad = ((ga0, ga1), (gb0, gb1))
    rfold = ((rfa0, rfa1), (rfb0, rfb1))
    above = ((upa0, upa1), (upb0, upb1))
    cleft = ((cla0, cla1), (clb0, clb1))
    cright = (cr0, cr1)
    taken = [0]
    started = []

    def send(src, dst, device):
        i = taken[0]
        taken[0] += 1
        copy = pltpu.make_async_remote_copy(
            src_ref=src, dst_ref=dst, send_sem=ssem.at[i], recv_sem=rsem.at[i],
            device_id=device, device_id_type=MESH,
        )
        copy.start()
        started.append(copy)
        return copy

    def strip(ways, land, way, turn, blocks):
        base = ways[0]
        ends = spot == turn
        for b, src in blocks:
            far = ends if b else False
            i = taken[0]
            taken[0] += 1
            hops = jnp.where(far, -2 * b * way, way)
            copy = pltpu.make_async_remote_copy(
                src_ref=src, dst_ref=land.at[jnp.where(far, 1, 0), b],
                send_sem=ssem.at[i],
                recv_sem=vsem.at[jnp.where(far, 1, 0), base + b],
                device_id=at_row(hops), device_id_type=MESH,
            )
            copy.start()
            started.append(copy)

    def hop(ways, land, way, turn):
        base, k = ways
        for b in (1, 2):
            @pl.when(spot == turn - 2 * b * way)
            def _():
                copy = pltpu.make_async_remote_copy(
                    src_ref=land.at[1, b], dst_ref=land.at[1, b],
                    send_sem=vsem.at[2, k], recv_sem=vsem.at[1, base + b],
                    device_id=at_row((2 * b + 1) * way), device_id_type=MESH,
                )
                copy.wait_recv()
                pltpu.make_async_remote_copy(
                    src_ref=land.at[1, b], dst_ref=land.at[0, b],
                    send_sem=vsem.at[2, k], recv_sem=vsem.at[0, base + b],
                    device_id=at_row((2 * b + 1) * way), device_id_type=MESH,
                ).start()
        hops_made.append((ways, land, way, turn))

    def hop_end(ways, land, way, turn):
        base, k = ways
        for b in (1, 2):
            @pl.when(spot == turn - 2 * b * way)
            def _():
                pltpu.make_async_remote_copy(
                    src_ref=land.at[1, b], dst_ref=land.at[0, b],
                    send_sem=vsem.at[2, k], recv_sem=vsem.at[0, base + b],
                    device_id=at_row((2 * b + 1) * way), device_id_type=MESH,
                ).wait_send()

    def landed(ways, land, blocks):
        for b in blocks:
            pltpu.make_async_remote_copy(
                src_ref=land.at[0, b], dst_ref=land.at[0, b],
                send_sem=vsem.at[2, ways[1]], recv_sem=vsem.at[0, ways[0] + b],
                device_id=at_row(1), device_id_type=MESH,
            ).wait_recv()

    hops_made = []
    UP, DOWN = (-1, 0), (1, RUN - 1)

    def ways_of(kind, t, s):
        k = (kind * 2 + t) * 2 + s
        return 3 * k, k

    barrier = pltpu.get_barrier_semaphore()
    near = [at_row(d * k) for k in range(1, 6) for d in (-1, 1)]
    for d in near + [left, right]:
        pl.semaphore_signal(barrier, inc=1, device_id=d, device_id_type=MESH)
    pl.semaphore_wait(barrier, len(near) + 2)

    lo, hi, all_rows, over = pl.ds(0, W), pl.ds(W, W), pl.ds(0, TILE), pl.ds(TILE, W)

    halo = []
    for s in range(2):
        strip(ways_of(0, 0, s), above[0][s], *UP, ((0, x.at[s, :, lo, lo]), (1, x.at[s, :, lo, hi])))
    for s in range(2):
        halo.append(send(x.at[s, :, lo, lo], ext[0][s].at[:, 2, lo], left))
    rest = [send(x.at[s, :, hi, lo], ext[0][s].at[:, 2, hi], left) for s in range(2)]

    for s in range(2):
        for b in range(2):
            ext[0][s][:, b, 0:TILE, :] = x[s, :, :, b * W:(b + 1) * W]
    pad[:, :, :, 0:TILE, :] = jnp.zeros((SLOTS, 2, 3, TILE, W), F32)
    pad[:, :, :, TILE + W:, :] = jnp.zeros((SLOTS, 2, 3, TILE, W), F32)
    for i in range(2):
        p = probe_in[i]
        prb[i * W:(i + 1) * W, :] = jnp.concatenate([p, p], 1)
    cs, sn = jnp.cos(phase[...]), jnp.sin(phase[...])
    prp[0:W, :] = jnp.concatenate([cs, cs], 1)
    prp[W:, :] = jnp.concatenate([sn, sn], 1)

    def corner(s):
        halo[s].wait_recv()
        strip(ways_of(0, 0, s), above[0][s], *UP, ((2, ext[0][s].at[:, 2, lo]),))

    def extend(t, s):
        ways = ways_of(0, t, s)
        landed(ways, above[t][s], range(3))
        for b in range(3):
            ext[t][s][:, b, TILE:, :] = above[t][s][0, b]

    def hop_up(t, s):
        hop(ways_of(0, t, s), above[t][s], *UP)

    def hop_down(t, s):
        hop(ways_of(1, t, s), rfold[t][s], *DOWN)

    lane = lax.broadcasted_iota(jnp.int32, (W, W), 1)

    def place(j):
        r, c = pos[0, j], pos[1, j]
        h = lax.shift_right_logical(c, 7)
        return r, h, c - h * W

    def window(e, j):
        r, h, s = place(j)
        back = lax.rem(W - s, W)
        parts = []
        for i in range(2):
            a = pltpu.roll(e[i, h, pl.ds(r, W), :], back, 1)
            b = pltpu.roll(e[i, h + 1, pl.ds(r, W), :], back, 1)
            parts.append(jnp.where(lane < W - s, a, b))
        return jnp.concatenate(parts, 0)

    def pair_window(e, p):
        return jnp.concatenate([window(e, 2 * p), window(e, 2 * p + 1)], 1)

    def spread(g, p):
        for k in range(2):
            j = 2 * p + k
            r, h, s = place(j)
            live = j < cnt[0]
            for i in range(2):
                v = pltpu.roll(g[i * W:(i + 1) * W, k * W:(k + 1) * W], s, 1)
                v = jnp.where(live, v, 0.0)
                first = jnp.where(lane >= s, v, 0.0)
                second = jnp.where(lane >= s, 0.0, v)
                pad[j, i, 0, over, :] = jnp.where(h == 0, first, 0.0)
                pad[j, i, 1, over, :] = jnp.where(h == 0, second, first)
                pad[j, i, 2, over, :] = jnp.where(h == 0, 0.0, second)

    def collect(g):
        starts = [TILE - place(j)[0] for j in range(SLOTS)]
        for i in range(2):
            for b in range(3):
                v = pad[0, i, b, pl.ds(starts[0], TILE + W), :]
                for j in range(1, SLOTS):
                    v = v + pad[j, i, b, pl.ds(starts[j], TILE + W), :]
                g[i, b] = v

    def fwd(v):
        return transform(v, (th[1], tl[1]), (th[0], tl[0]))

    def bwd(v):
        return transform(v, (th[0], tl[0]), (th[1], tl[1]))

    def phase_a(e):
        for p in range(2):
            v = fwd(cmul(prb[...], pair_window(e, p)))
            q_s[p] = bwd(cmul(prp[...], v))

    def phase_b(e, g):
        for p in range(2):
            o2 = pair_window(e, p)
            o2_s[p] = o2
            psi = fwd(cmul(q_s[p], o2))
            pr, pi = psi[:W], psi[W:]
            m = jnp.concatenate([amp[order[2 * p]], amp[order[2 * p + 1]]], 1)
            f = 1.0 - m / jnp.maximum(jnp.sqrt(pr * pr + pi * pi), FLOOR)
            d2 = bwd(jnp.concatenate([pr * f, pi * f], 0))
            spread(cmul_conj(q_s[p], d2), p)
            back_s[p] = cmul_conj(o2_s[p], d2)
        collect(g)

    def phase_c(g):
        for p in range(2):
            v = bwd(cmul_conj(prp[...], fwd(back_s[p])))
            spread(cmul_conj(prb[...], v), p)
        collect(g)

    def fold_start(t, s):
        g = grad[t][s]
        strip(ways_of(1, t, s), rfold[t][s], *DOWN, [(b, g.at[:, b, over]) for b in range(3)])

    def trade(t, s, rows):
        g = grad[t][s]
        cs = [send(g.at[:, 2, rows], cleft[t][s].at[:, rows], right)]
        if t == 0:
            cs.append(send(g.at[:, 0, rows], cright[s].at[:, rows], left))
        return cs

    def fold_in(t, s, blocks):
        g = grad[t][s]
        landed(ways_of(1, t, s), rfold[t][s], blocks)
        for b in blocks:
            g[:, b, 0:W, :] += rfold[t][s][0, b]

    def fold_end(t, s):
        fold_in(t, s, (0, 2) if t == 0 else (2,))

    def update(s, half, cs):
        for c in cs:
            c.wait_recv()
        a, b = half * W, half * W + W
        e, g, n = ext[0][s], grad[0][s], ext[1][s]
        n[:, 0, a:b, :] = e[:, 0, a:b, :] - STEP * (g[:, 0, a:b, :] + cleft[0][s][:, a:b, :])
        n[:, 1, a:b, :] = e[:, 1, a:b, :] - STEP * g[:, 1, a:b, :]
        n[:, 2, a:b, :] = e[:, 2, a:b, :] - STEP * (g[:, 2, a:b, :] + cright[s][:, a:b, :])

    def finish(s, half, cs):
        for c in cs:
            c.wait_recv()
        a, b = half * W, half * W + W
        e, g = ext[1][s], grad[1][s]
        out[s, :, a:b, 0:W] = e[:, 0, a:b, :] - STEP * (g[:, 0, a:b, :] + cleft[1][s][:, a:b, :])
        out[s, :, a:b, W:] = e[:, 1, a:b, :] - STEP * g[:, 1, a:b, :]

    def lower(s, lows):
        fold_in(0, s, (1,))
        update(s, 0, lows)
        strip(ways_of(0, 1, s), above[1][s], *UP, [(b, ext[1][s].at[:, b, lo]) for b in range(3)])

    corner(0)
    corner(1)
    hop_up(0, 0)
    hop_up(0, 1)
    rest[0].wait_recv()
    extend(0, 0)
    phase_a(ext[0][0])
    rest[1].wait_recv()
    extend(0, 1)
    phase_b(ext[0][1], grad[0][1])
    fold_start(0, 1)
    h1 = trade(0, 1, pl.ds(W, W // 2))
    phase_c(grad[0][0])
    fold_start(0, 0)
    hop_down(0, 1)
    hop_down(0, 0)
    fold_end(0, 0)
    l0 = trade(0, 0, lo)
    fold_end(0, 1)
    l1 = trade(0, 1, lo)
    h0 = trade(0, 0, hi)
    k1 = trade(0, 1, pl.ds(W + W // 2, W // 2))
    lower(0, l0)
    lower(1, l1)
    hop_up(1, 0)
    hop_up(1, 1)
    update(0, 1, h0)
    extend(1, 0)
    phase_a(ext[1][0])
    update(1, 1, h1 + k1)
    extend(1, 1)
    phase_b(ext[1][1], grad[1][1])
    fold_start(1, 1)
    h1 = trade(1, 1, hi)
    phase_c(grad[1][0])
    fold_start(1, 0)
    h0 = trade(1, 0, hi)
    hop_down(1, 1)
    hop_down(1, 0)
    fold_end(1, 1)
    l1 = trade(1, 1, lo)
    fold_end(1, 0)
    l0 = trade(1, 0, lo)
    finish(1, 1, h1)
    finish(0, 1, h0)
    fold_in(1, 1, (0, 1))
    finish(1, 0, l1)
    fold_in(1, 0, (0, 1))
    finish(0, 0, l0)
    for c in started:
        c.wait_send()
    for h in hops_made:
        hop_end(*h)


COPIES = 60


def body(specimen, probe, phase, amplitudes, positions, counts, order):
    th, tl = tables()
    ext = pltpu.VMEM((2, 3, TILE + W, W), F32)
    edge = pltpu.VMEM((2, 3, 2, W, W), F32)
    strip = pltpu.VMEM((2, TILE, W), F32)
    wave = pltpu.VMEM((2, 2 * W, 2 * W), F32)
    vmem = pl.BlockSpec(memory_space=pltpu.VMEM)
    smem = pl.BlockSpec(memory_space=pltpu.SMEM)
    return pl.pallas_call(
        kernel,
        out_shape=jax.ShapeDtypeStruct(specimen.shape, F32),
        in_specs=[smem] * 3 + [vmem] * 6,
        out_specs=vmem,
        scratch_shapes=[ext] * 8 + [edge] * 8 + [strip] * 6
        + [
            pltpu.VMEM((SLOTS, 2, 3, 2 * TILE + W, W), F32),
            pltpu.VMEM((2 * W, 2 * W), F32),
            pltpu.VMEM((2 * W, 2 * W), F32),
            wave, wave, wave,
            pltpu.SemaphoreType.DMA((COPIES,)),
            pltpu.SemaphoreType.DMA((COPIES,)),
            pltpu.SemaphoreType.DMA((3, 24)),
        ],
        compiler_params=pltpu.CompilerParams(
            collective_id=0, has_side_effects=True, vmem_limit_bytes=56 * 2**20
        ),
    )(
        positions[0, 0].T, counts[0], order[0, 0],
        specimen, probe, phase, amplitudes[0, 0], th, tl,
    )


def solution(mesh):
    placed = (
        P(None, None, "row", "col"),
        P(),
        P(),
        P("row", "col", None, None, None),
        P("row", "col", None, None),
        P("row", "col"),
        P("row", "col", None),
    )
    return jax.shard_map(
        body, mesh=mesh, in_specs=placed, out_specs=P(None, None, "row", "col"), check_vma=False
    )
```

```python
import math

import jax
import jax.numpy as jnp
import numpy as np
from jax import lax
from jax.experimental import pallas as pl
from jax.experimental.pallas import tpu as pltpu
from jax.sharding import PartitionSpec as P

SLOTS = 4
RUN = 8
W = 128
TILE = 256
STEP = 0.02
FLOOR = 0.5
F32 = jnp.float32
BF16 = jnp.bfloat16
MESH = pl.DeviceIdType.MESH


def tables():
    k = np.arange(W)
    angle = (k[:, None] * k[None, :] % W) * (2.0 * math.pi / W)
    re = np.cos(angle) / math.sqrt(W)
    im = -np.sin(angle) / math.sqrt(W)
    forward = np.block([[re, im], [-im, re]]).astype(np.float32)
    backward = np.block([[re, -im], [im, re]]).astype(np.float32)
    both = jnp.asarray(np.stack([forward, backward]))
    high = both.astype(BF16)
    low = (both - high.astype(F32)).astype(BF16)
    return high, low


def split(v):
    high = v.astype(BF16)
    return high, (v - high.astype(F32)).astype(BF16)


def dot(a, b):
    return jnp.dot(a, b, preferred_element_type=F32)


def swap_blocks(v):
    top = jnp.concatenate([v[:W, :W], v[W:, :W]], 1)
    bottom = jnp.concatenate([v[:W, W:], v[W:, W:]], 1)
    return jnp.concatenate([top, bottom], 0)


def transform(v, left, right):
    vh, vl = split(v)
    v = dot(left[0], vh) + (dot(left[1], vh) + dot(left[0], vl))
    vh, vl = split(swap_blocks(v))
    v = dot(vh, right[0]) + (dot(vh, right[1]) + dot(vl, right[0]))
    return swap_blocks(v)


def cmul(a, b):
    ar, ai, br, bi = a[:W], a[W:], b[:W], b[W:]
    return jnp.concatenate([ar * br - ai * bi, ar * bi + ai * br], 0)


def cmul_conj(a, b):
    ar, ai, br, bi = a[:W], a[W:], b[:W], b[W:]
    return jnp.concatenate([ar * br + ai * bi, ar * bi - ai * br], 0)


def kernel(
    pos, cnt, order,
    x, probe_in, phase, amp, th, tl,
    out,
    ea0, ea1, eb0, eb1, ga0, ga1, gb0, gb1,
    rfa0, rfa1, rfb0, rfb1, upa0, upa1, upb0, upb1, cla0, cla1, clb0, clb1, cr0, cr1,
    pad, prb, prp, q_s, o2_s, back_s,
    ssem, rsem, vsem,
):
    row, col = lax.axis_index("row"), lax.axis_index("col")
    n_row, n_col = lax.axis_size("row"), lax.axis_size("col")
    spot = lax.rem(row, RUN)

    def at_row(distance):
        return (lax.rem(row + n_row + distance, n_row), col)

    left = (row, lax.rem(col + n_col - 1, n_col))
    right = (row, lax.rem(col + 1, n_col))
    ext = ((ea0, ea1), (eb0, eb1))
    grad = ((ga0, ga1), (gb0, gb1))
    rfold = ((rfa0, rfa1), (rfb0, rfb1))
    above = ((upa0, upa1), (upb0, upb1))
    cleft = ((cla0, cla1), (clb0, clb1))
    cright = (cr0, cr1)
    taken = [0]
    started = []

    def send(src, dst, device):
        i = taken[0]
        taken[0] += 1
        copy = pltpu.make_async_remote_copy(
            src_ref=src, dst_ref=dst, send_sem=ssem.at[i], recv_sem=rsem.at[i],
            device_id=device, device_id_type=MESH,
        )
        copy.start()
        started.append(copy)
        return copy

    def strip(ways, land, way, turn, blocks):
        base = ways[0]
        ends = spot == turn
        for b, src in blocks:
            far = ends if b else False
            i = taken[0]
            taken[0] += 1
            hops = jnp.where(far, -2 * b * way, way)
            copy = pltpu.make_async_remote_copy(
                src_ref=src, dst_ref=land.at[jnp.where(far, 1, 0), b],
                send_sem=ssem.at[i],
                recv_sem=vsem.at[jnp.where(far, 1, 0), base + b],
                device_id=at_row(hops), device_id_type=MESH,
            )
            copy.start()
            started.append(copy)

    def hop(ways, land, way, turn):
        base, k = ways
        for b in (1, 2):
            @pl.when(spot == turn - 2 * b * way)
            def _():
                copy = pltpu.make_async_remote_copy(
                    src_ref=land.at[1, b], dst_ref=land.at[1, b],
                    send_sem=vsem.at[2, k], recv_sem=vsem.at[1, base + b],
                    device_id=at_row((2 * b + 1) * way), device_id_type=MESH,
                )
                copy.wait_recv()
                pltpu.make_async_remote_copy(
                    src_ref=land.at[1, b], dst_ref=land.at[0, b],
                    send_sem=vsem.at[2, k], recv_sem=vsem.at[0, base + b],
                    device_id=at_row((2 * b + 1) * way), device_id_type=MESH,
                ).start()
        hops_made.append((ways, land, way, turn))

    def hop_end(ways, land, way, turn):
        base, k = ways
        for b in (1, 2):
            @pl.when(spot == turn - 2 * b * way)
            def _():
                pltpu.make_async_remote_copy(
                    src_ref=land.at[1, b], dst_ref=land.at[0, b],
                    send_sem=vsem.at[2, k], recv_sem=vsem.at[0, base + b],
                    device_id=at_row((2 * b + 1) * way), device_id_type=MESH,
                ).wait_send()

    def landed(ways, land, blocks):
        for b in blocks:
            pltpu.make_async_remote_copy(
                src_ref=land.at[0, b], dst_ref=land.at[0, b],
                send_sem=vsem.at[2, ways[1]], recv_sem=vsem.at[0, ways[0] + b],
                device_id=at_row(1), device_id_type=MESH,
            ).wait_recv()

    hops_made = []
    UP, DOWN = (-1, 0), (1, RUN - 1)

    def ways_of(kind, t, s):
        k = (kind * 2 + t) * 2 + s
        return 3 * k, k

    barrier = pltpu.get_barrier_semaphore()
    near = [at_row(d * k) for k in range(1, 6) for d in (-1, 1)]
    for d in near + [left, right]:
        pl.semaphore_signal(barrier, inc=1, device_id=d, device_id_type=MESH)
    pl.semaphore_wait(barrier, len(near) + 2)

    lo, hi, all_rows, over = pl.ds(0, W), pl.ds(W, W), pl.ds(0, TILE), pl.ds(TILE, W)

    halo = []
    for s in range(2):
        e = ext[0][s]
        c0 = send(x.at[s, :, lo, lo], e.at[:, 2, lo], left)
        halo.append(c0)
        strip(ways_of(0, 0, s), above[0][s], *UP, ((0, x.at[s, :, lo, lo]), (1, x.at[s, :, lo, hi])))

    rest = [send(x.at[s, :, hi, lo], ext[0][s].at[:, 2, hi], left) for s in range(2)]

    for s in range(2):
        for b in range(2):
            ext[0][s][:, b, 0:TILE, :] = x[s, :, :, b * W:(b + 1) * W]
    pad[:, :, :, 0:TILE, :] = jnp.zeros((SLOTS, 2, 3, TILE, W), F32)
    pad[:, :, :, TILE + W:, :] = jnp.zeros((SLOTS, 2, 3, TILE, W), F32)
    for i in range(2):
        p = probe_in[i]
        prb[i * W:(i + 1) * W, :] = jnp.concatenate([p, p], 1)
    cs, sn = jnp.cos(phase[...]), jnp.sin(phase[...])
    prp[0:W, :] = jnp.concatenate([cs, cs], 1)
    prp[W:, :] = jnp.concatenate([sn, sn], 1)

    def corner(s):
        halo[s].wait_recv()
        strip(ways_of(0, 0, s), above[0][s], *UP, ((2, ext[0][s].at[:, 2, lo]),))

    def extend(t, s):
        ways = ways_of(0, t, s)
        landed(ways, above[t][s], range(3))
        for b in range(3):
            ext[t][s][:, b, TILE:, :] = above[t][s][0, b]

    def hop_up(t, s):
        hop(ways_of(0, t, s), above[t][s], *UP)

    def hop_down(t, s):
        hop(ways_of(1, t, s), rfold[t][s], *DOWN)

    lane = lax.broadcasted_iota(jnp.int32, (W, W), 1)

    def place(j):
        r, c = pos[0, j], pos[1, j]
        h = lax.shift_right_logical(c, 7)
        return r, h, c - h * W

    def window(e, j):
        r, h, s = place(j)
        back = lax.rem(W - s, W)
        parts = []
        for i in range(2):
            a = pltpu.roll(e[i, h, pl.ds(r, W), :], back, 1)
            b = pltpu.roll(e[i, h + 1, pl.ds(r, W), :], back, 1)
            parts.append(jnp.where(lane < W - s, a, b))
        return jnp.concatenate(parts, 0)

    def pair_window(e, p):
        return jnp.concatenate([window(e, 2 * p), window(e, 2 * p + 1)], 1)

    def spread(g, p):
        for k in range(2):
            j = 2 * p + k
            r, h, s = place(j)
            live = j < cnt[0]
            for i in range(2):
                v = pltpu.roll(g[i * W:(i + 1) * W, k * W:(k + 1) * W], s, 1)
                v = jnp.where(live, v, 0.0)
                first = jnp.where(lane >= s, v, 0.0)
                second = jnp.where(lane >= s, 0.0, v)
                pad[j, i, 0, over, :] = jnp.where(h == 0, first, 0.0)
                pad[j, i, 1, over, :] = jnp.where(h == 0, second, first)
                pad[j, i, 2, over, :] = jnp.where(h == 0, 0.0, second)

    def collect(g):
        starts = [TILE - place(j)[0] for j in range(SLOTS)]
        for i in range(2):
            for b in range(3):
                v = pad[0, i, b, pl.ds(starts[0], TILE + W), :]
                for j in range(1, SLOTS):
                    v = v + pad[j, i, b, pl.ds(starts[j], TILE + W), :]
                g[i, b] = v

    def fwd(v):
        return transform(v, (th[1], tl[1]), (th[0], tl[0]))

    def bwd(v):
        return transform(v, (th[0], tl[0]), (th[1], tl[1]))

    def phase_a(e):
        for p in range(2):
            v = fwd(cmul(prb[...], pair_window(e, p)))
            q_s[p] = bwd(cmul(prp[...], v))

    def phase_b(e, g):
        for p in range(2):
            o2 = pair_window(e, p)
            o2_s[p] = o2
            psi = fwd(cmul(q_s[p], o2))
            pr, pi = psi[:W], psi[W:]
            m = jnp.concatenate([amp[order[2 * p]], amp[order[2 * p + 1]]], 1)
            f = 1.0 - m / jnp.maximum(jnp.sqrt(pr * pr + pi * pi), FLOOR)
            d2 = bwd(jnp.concatenate([pr * f, pi * f], 0))
            spread(cmul_conj(q_s[p], d2), p)
            back_s[p] = cmul_conj(o2_s[p], d2)
        collect(g)

    def phase_c(g):
        for p in range(2):
            v = bwd(cmul_conj(prp[...], fwd(back_s[p])))
            spread(cmul_conj(prb[...], v), p)
        collect(g)

    def fold_start(t, s):
        g = grad[t][s]
        strip(ways_of(1, t, s), rfold[t][s], *DOWN, [(b, g.at[:, b, over]) for b in range(3)])

    def trade(t, s, rows):
        g = grad[t][s]
        cs = [send(g.at[:, 2, rows], cleft[t][s].at[:, rows], right)]
        if t == 0:
            cs.append(send(g.at[:, 0, rows], cright[s].at[:, rows], left))
        return cs

    def fold_end(t, s):
        g = grad[t][s]
        landed(ways_of(1, t, s), rfold[t][s], range(3))
        for b in range(3):
            g[:, b, 0:W, :] += rfold[t][s][0, b]

    def update(s, half, cs):
        for c in cs:
            c.wait_recv()
        a, b = half * W, half * W + W
        e, g, n = ext[0][s], grad[0][s], ext[1][s]
        n[:, 0, a:b, :] = e[:, 0, a:b, :] - STEP * (g[:, 0, a:b, :] + cleft[0][s][:, a:b, :])
        n[:, 1, a:b, :] = e[:, 1, a:b, :] - STEP * g[:, 1, a:b, :]
        n[:, 2, a:b, :] = e[:, 2, a:b, :] - STEP * (g[:, 2, a:b, :] + cright[s][:, a:b, :])

    def finish(s, half, cs):
        for c in cs:
            c.wait_recv()
        a, b = half * W, half * W + W
        e, g = ext[1][s], grad[1][s]
        out[s, :, a:b, 0:W] = e[:, 0, a:b, :] - STEP * (g[:, 0, a:b, :] + cleft[1][s][:, a:b, :])
        out[s, :, a:b, W:] = e[:, 1, a:b, :] - STEP * g[:, 1, a:b, :]

    def lower(s, lows):
        update(s, 0, lows)
        strip(ways_of(0, 1, s), above[1][s], *UP, [(b, ext[1][s].at[:, b, lo]) for b in range(3)])

    corner(0)
    corner(1)
    hop_up(0, 0)
    hop_up(0, 1)
    rest[0].wait_recv()
    extend(0, 0)
    phase_a(ext[0][0])
    rest[1].wait_recv()
    extend(0, 1)
    phase_b(ext[0][1], grad[0][1])
    fold_start(0, 1)
    h1 = trade(0, 1, pl.ds(W, W // 2))
    phase_c(grad[0][0])
    fold_start(0, 0)
    hop_down(0, 1)
    hop_down(0, 0)
    fold_end(0, 0)
    l0 = trade(0, 0, lo)
    fold_end(0, 1)
    l1 = trade(0, 1, lo)
    h0 = trade(0, 0, hi)
    lower(0, l0)
    k1 = trade(0, 1, pl.ds(W + W // 2, W // 2))
    lower(1, l1)
    hop_up(1, 0)
    hop_up(1, 1)
    update(0, 1, h0)
    extend(1, 0)
    phase_a(ext[1][0])
    update(1, 1, h1 + k1)
    extend(1, 1)
    phase_b(ext[1][1], grad[1][1])
    fold_start(1, 1)
    h1 = trade(1, 1, hi)
    phase_c(grad[1][0])
    fold_start(1, 0)
    h0 = trade(1, 0, hi)
    hop_down(1, 1)
    hop_down(1, 0)
    fold_end(1, 1)
    l1 = trade(1, 1, lo)
    fold_end(1, 0)
    l0 = trade(1, 0, lo)
    finish(1, 1, h1)
    finish(0, 1, h0)
    finish(1, 0, l1)
    finish(0, 0, l0)
    for c in started:
        c.wait_send()
    for h in hops_made:
        hop_end(*h)


COPIES = 60


def body(specimen, probe, phase, amplitudes, positions, counts, order):
    th, tl = tables()
    ext = pltpu.VMEM((2, 3, TILE + W, W), F32)
    edge = pltpu.VMEM((2, 3, 2, W, W), F32)
    strip = pltpu.VMEM((2, TILE, W), F32)
    wave = pltpu.VMEM((2, 2 * W, 2 * W), F32)
    vmem = pl.BlockSpec(memory_space=pltpu.VMEM)
    smem = pl.BlockSpec(memory_space=pltpu.SMEM)
    return pl.pallas_call(
        kernel,
        out_shape=jax.ShapeDtypeStruct(specimen.shape, F32),
        in_specs=[smem] * 3 + [vmem] * 6,
        out_specs=vmem,
        scratch_shapes=[ext] * 8 + [edge] * 8 + [strip] * 6
        + [
            pltpu.VMEM((SLOTS, 2, 3, 2 * TILE + W, W), F32),
            pltpu.VMEM((2 * W, 2 * W), F32),
            pltpu.VMEM((2 * W, 2 * W), F32),
            wave, wave, wave,
            pltpu.SemaphoreType.DMA((COPIES,)),
            pltpu.SemaphoreType.DMA((COPIES,)),
            pltpu.SemaphoreType.DMA((3, 24)),
        ],
        compiler_params=pltpu.CompilerParams(
            collective_id=0, has_side_effects=True, vmem_limit_bytes=56 * 2**20
        ),
    )(
        positions[0, 0].T, counts[0], order[0, 0],
        specimen, probe, phase, amplitudes[0, 0], th, tl,
    )


def solution(mesh):
    placed = (
        P(None, None, "row", "col"),
        P(),
        P(),
        P("row", "col", None, None, None),
        P("row", "col", None, None),
        P("row", "col"),
        P("row", "col", None),
    )
    return jax.shard_map(
        body, mesh=mesh, in_specs=placed, out_specs=P(None, None, "row", "col"), check_vma=False
    )
```
